32 devices in a mesh: group: 2 (over y), gx: 4 (over z), gy: 4 (over x, core).
Axes of the slice: x: 2, y: 2, z: 4, core: 2. Of those that a mesh axis runs over, the one named last changes fastest.
Arguments:
- displacement: float32 [2, 3, 32, 64, 128], P('group', None, 'gx', 'gy'), may hold values from -6 to 6
- velocity: float32 [2, 3, 32, 64, 128], P('group', None, 'gx', 'gy'), may hold values from -6 to 6
- modulus: float32 [2, 32, 64, 128], P('group', 'gx', 'gy'), may hold values from 1 to 4
- bond_words: int32 [2, 32, 64, 128], P(None, 'gx', 'gy'), may hold values from 0 to 2147483647, as said below
- coupling_map: int32 [3, 32, 64], P(None, 'gx', 'gy'), may hold values from 0 to 2
Outputs:
- new_displacement: float32 [2, 3, 32, 64, 128], P('group', None, 'gx', 'gy')
- new_velocity: float32 [2, 3, 32, 64, 128], P('group', None, 'gx', 'gy')
The draws below stay inside these ranges and needn't reach their ends.
Inputs may be any that keep to these rules, and one draw needn't show every extreme that they name: `bond_words`: bonds to positions outside the zone are 0; bit 30 of word 1 is 0.
All inputs are finite; a program needn't handle non-finite values.
Results may differ from the reference program's by a relative error of at most 0.0001.
Values sent between devices are 32-bit elements; how exact they have to be, the bound alone decides.
A program may use at most 64 MiB of HBM per device.

```python
import math
import jax
import jax.numpy as jnp
import numpy as np
from jax import lax

NZ = 128
OV = 3
STEPS = 1
NX = 32
NY = 64


def half_offsets_drawn():
    table = []
    for delta_x in range(-3, 4):
        for delta_y in range(-3, 4):
            for delta_z in range(-3, 4):
                radius = delta_x * delta_x + delta_y * delta_y + delta_z * delta_z
                if 0 < radius <= 9 and (delta_x, delta_y, delta_z) > (0, 0, 0):
                    table.append((delta_x, delta_y, delta_z))
    return table


def draw_bond_words(key, part):
    grid_x = jnp.arange(NX)[:, None, None]
    grid_y = jnp.arange(NY)[None, :, None]
    grid_z = jnp.arange(NZ)[None, None, :]
    packed = [jnp.zeros((NX, NY, NZ), jnp.int32), jnp.zeros((NX, NY, NZ), jnp.int32)]
    for number, offset in enumerate(half_offsets_drawn()):
        delta_x, delta_y, delta_z = offset
        intact = jax.random.randint(jax.random.fold_in(key, number), (NX, NY, NZ), 0, 4) > 0
        inside = (grid_x + delta_x >= 0) & (grid_x + delta_x < NX) & (grid_y + delta_y >= 0) & (grid_y + delta_y < NY) & (grid_z + delta_z >= 0) & (grid_z + delta_z < NZ)
        crack = (grid_x < NX // 2) & (grid_x + delta_x >= NX // 2) & (grid_y < NY // 2)
        flagged = (intact & inside & ~crack).astype(jnp.int32)
        packed[number // 31] = packed[number // 31] + flagged * (1 << number % 31)
    return jnp.stack(packed)


def touch_ends(values, stream_key, least, largest):
    place = [jax.random.randint(jax.random.fold_in(stream_key, axis), (), 0, length) for axis, length in enumerate(values.shape)]
    widest = values.shape.index(max(values.shape))
    beside = place[:widest] + [(place[widest] + 1) % values.shape[widest]] + place[widest + 1:]
    return values.at[tuple(place)].set(least).at[tuple(beside)].set(largest)


def steps_of(rng, extent, split, low, top_value):
    def one(position, blocks):
        draws = jax.random.uniform(jax.random.fold_in(jax.random.fold_in(rng, 6), position), (blocks,), jnp.float32, low / len(split), top_value / len(split))
        return jnp.repeat(jnp.exp(draws), extent[position] // blocks).reshape((-1,) + (1,) * (len(extent) - position - 1))

    loudness = one(*split[0])
    for cut in split[1:]:
        loudness = loudness * one(*cut)
    return loudness


def noise(key, dims, scale, most, cuts=(), kind=jnp.bfloat16):
    values = scale * jax.random.normal(key, dims, jnp.float32)
    if cuts:
        values = values * steps_of(key, dims, cuts, -0.22, 0.18)
    return jnp.clip(values, -most, most).astype(kind)


def setup_inputs(seed: int = 0) -> dict:
    seeds = jax.random.split(jax.random.key(seed), 6)
    return {
        "displacement": noise(seeds[0], (2, 3, NX, NY, NZ), 1.0, 6.0, ((0, 2), (2, 4), (3, 4)), jnp.float32),
        "velocity": noise(seeds[1], (2, 3, NX, NY, NZ), 1.0, 6.0, ((0, 2), (2, 4), (3, 4)), jnp.float32),
        "modulus": jnp.clip(jnp.exp(math.log(4.0) - 1.3862944 * jax.random.uniform(seeds[2], (2, NX, NY, NZ), jnp.float32) ** steps_of(seeds[2], (2, NX, NY, NZ), ((0, 2), (1, 4), (2, 4)), -0.2, 0.2)), 1.0, 4.0),
        "bond_words": draw_bond_words(jax.random.fold_in(seeds[5], 71), 0),
        "coupling_map": touch_ends(jax.random.randint(seeds[4], (OV, NX, NY), 0, OV), jax.random.fold_in(seeds[4], 1), 0, OV - 1).astype(jnp.int32),
    }


time_step = 0.1
bond_scale = 1.0

def half_offsets():
    table = []
    for delta_x in range(-3, 4):
        for delta_y in range(-3, 4):
            for delta_z in range(-3, 4):
                radius = delta_x * delta_x + delta_y * delta_y + delta_z * delta_z
                if 0 < radius <= 9 and (delta_x, delta_y, delta_z) > (0, 0, 0):
                    table.append((delta_x, delta_y, delta_z))
    return table

def hex_stiffness():
    poisson = 0.3
    lame_first = poisson / ((1.0 + poisson) * (1.0 - 2.0 * poisson))
    shear_modulus = 0.5 / (1.0 + poisson)
    elastic = np.zeros((6, 6))
    elastic[:3, :3] = lame_first
    for axis_id in range(3):
        elastic[axis_id, axis_id] += 2.0 * shear_modulus
        elastic[3 + axis_id, 3 + axis_id] = shear_modulus
    points = [0.5 - 0.5 / math.sqrt(3.0), 0.5 + 0.5 / math.sqrt(3.0)]
    result = np.zeros((24, 24))
    shear_pairs = ((0, 1), (1, 2), (0, 2))
    for along_x in points:
        for along_y in points:
            for along_z in points:
                coords = (along_x, along_y, along_z)
                gradients = np.zeros((3, 8))
                for corner in range(8):
                    corner_bits = (corner >> 2 & 1, corner >> 1 & 1, corner & 1)
                    factors = [coords[axis_id] if corner_bits[axis_id] else 1.0 - coords[axis_id] for axis_id in range(3)]
                    slopes = [1.0 if corner_bits[axis_id] else -1.0 for axis_id in range(3)]
                    gradients[0, corner] = slopes[0] * factors[1] * factors[2]
                    gradients[1, corner] = factors[0] * slopes[1] * factors[2]
                    gradients[2, corner] = factors[0] * factors[1] * slopes[2]
                strain = np.zeros((6, 24))
                for axis_id in range(3):
                    strain[axis_id, axis_id * 8:axis_id * 8 + 8] = gradients[axis_id]
                for shear_row, pair in enumerate(shear_pairs):
                    left_axis, right_axis = pair
                    strain[3 + shear_row, left_axis * 8:left_axis * 8 + 8] = gradients[right_axis]
                    strain[3 + shear_row, right_axis * 8:right_axis * 8 + 8] = gradients[left_axis]
                result += strain.T @ elastic @ strain / 8.0
    return result

def bond_sum(field_pad, words_pad, modulus_pad, size_x, size_y, size_z):

    def window(array, delta_x, delta_y, delta_z):
        return array[..., 3 + delta_x:3 + delta_x + size_x, 3 + delta_y:3 + delta_y + size_y, 3 + delta_z:3 + delta_z + size_z]
    centre = window(field_pad, 0, 0, 0)
    centre_modulus = window(modulus_pad, 0, 0, 0)
    centre_words = window(words_pad, 0, 0, 0)
    summed = jnp.zeros_like(centre)
    for number, offset in enumerate(half_offsets()):
        delta_x, delta_y, delta_z = offset
        word_id = number // 31
        bit_id = number % 31
        factor = 0.5 * bond_scale / float(delta_x * delta_x + delta_y * delta_y + delta_z * delta_z) ** 1.5
        ahead_diff = window(field_pad, delta_x, delta_y, delta_z) - centre
        behind_diff = window(field_pad, -delta_x, -delta_y, -delta_z) - centre
        ahead_proj = delta_x * ahead_diff[0] + delta_y * ahead_diff[1] + delta_z * ahead_diff[2]
        behind_proj = delta_x * behind_diff[0] + delta_y * behind_diff[1] + delta_z * behind_diff[2]
        ahead_flag = (centre_words[word_id] >> bit_id & 1).astype(jnp.float32)
        behind_flag = (window(words_pad[word_id], -delta_x, -delta_y, -delta_z) >> bit_id & 1).astype(jnp.float32)
        strength = ahead_flag * (centre_modulus + window(modulus_pad, delta_x, delta_y, delta_z)) * ahead_proj
        strength = strength + behind_flag * (centre_modulus + window(modulus_pad, -delta_x, -delta_y, -delta_z)) * behind_proj
        strength = factor * strength
        summed = summed + jnp.stack([delta_x * strength, delta_y * strength, delta_z * strength])
    return summed

def couple(below_top, map_layers):
    coupled = jnp.zeros_like(below_top)
    for layer_id in range(below_top.shape[3]):
        coupled = coupled + jnp.where(map_layers[None] == layer_id, below_top[..., layer_id:layer_id + 1], 0.0)
    return coupled

def spread(reaction, map_layers):
    columns = []
    for layer_id in range(reaction.shape[3]):
        columns.append(lax.optimization_barrier(jnp.sum(jnp.where(map_layers[None] == layer_id, reaction, 0.0), axis=3)))
    return jnp.stack(columns, axis=3)

def slab_forces(field_now, modulus_slab):
    size_x, size_y, size_z = (field_now.shape[1], field_now.shape[2], field_now.shape[3])
    stiffness = jnp.asarray(hex_stiffness(), dtype=jnp.float32)
    field_pad = jnp.pad(field_now, ((0, 0), (0, 1), (0, 1), (0, 1)))
    pieces = []
    for component in range(3):
        for corner in range(8):
            corner_x, corner_y, corner_z = (corner >> 2 & 1, corner >> 1 & 1, corner & 1)
            pieces.append(field_pad[component, corner_x:corner_x + size_x, corner_y:corner_y + size_y, corner_z:corner_z + size_z])
    gathered = jnp.stack(pieces).reshape(24, -1)
    inside = ((jnp.arange(size_x) < size_x - 1)[:, None, None] & (jnp.arange(size_y) < size_y - 1)[None, :, None] & (jnp.arange(size_z) < size_z - 1)[None, None, :]).astype(jnp.float32)
    result = jnp.dot(stiffness, gathered, precision=lax.Precision.HIGHEST, preferred_element_type=jnp.float32)
    result = result.reshape(24, size_x, size_y, size_z) * (modulus_slab * inside)[None]
    result_pad = jnp.pad(result, ((0, 0), (1, 0), (1, 0), (1, 0)))
    forces = []
    for component in range(3):
        summed = jnp.zeros((size_x, size_y, size_z), jnp.float32)
        for corner in range(8):
            corner_x, corner_y, corner_z = (corner >> 2 & 1, corner >> 1 & 1, corner & 1)
            summed = summed - result_pad[component * 8 + corner, 1 - corner_x:1 - corner_x + size_x, 1 - corner_y:1 - corner_y + size_y, 1 - corner_z:1 - corner_z + size_z]
        forces.append(summed)
    return jnp.stack(forces)

def reference(displacement, velocity, modulus, bond_words, coupling_map):
    zone_field, slab_field = (displacement[0], displacement[1])
    zone_speed, slab_speed = (velocity[0], velocity[1])
    map_layers = jnp.transpose(coupling_map, (1, 2, 0))
    layer_ids = jnp.arange(NZ)
    moving = (layer_ids >= OV)[None, None, None, :]
    unclamped = (layer_ids > 0)[None, None, None, :]
    count_x = (jnp.arange(NX) > 0).astype(jnp.float32) + (jnp.arange(NX) < NX - 1).astype(jnp.float32)
    count_y = (jnp.arange(NY) > 0).astype(jnp.float32) + (jnp.arange(NY) < NY - 1).astype(jnp.float32)
    count_z = (layer_ids > 0).astype(jnp.float32) + (layer_ids < NZ - 1).astype(jnp.float32)
    lumped_mass = count_x[:, None, None] * count_y[None, :, None] * count_z[None, None, :] / 8.0
    words_pad = jnp.pad(bond_words, ((0, 0), (3, 3), (3, 3), (3, 3)))
    modulus_pad = jnp.pad(modulus[0], ((3, 3), (3, 3), (3, 3)))
    for step_count in range(STEPS):
        coupled = couple(slab_field[..., NZ - OV:], map_layers)
        zone_field = jnp.concatenate([coupled, zone_field[..., OV:]], axis=3)
        field_pad = jnp.pad(zone_field, ((0, 0), (3, 3), (3, 3), (3, 3)))
        zone_force = bond_sum(field_pad, words_pad, modulus_pad, NX, NY, NZ)
        interface = jnp.pad(spread(zone_force[..., :OV], map_layers), ((0, 0), (0, 0), (0, 0), (NZ - OV, 0)))
        slab_force = slab_forces(slab_field, modulus[1]) + interface
        zone_speed = jnp.where(moving, zone_speed + time_step * zone_force, zone_speed)
        zone_field = jnp.where(moving, zone_field + time_step * zone_speed, zone_field)
        slab_speed = jnp.where(unclamped, slab_speed + time_step * slab_force / lumped_mass, 0.0)
        slab_field = jnp.where(unclamped, slab_field + time_step * slab_speed, 0.0)
    return (jnp.stack([zone_field, slab_field]), jnp.stack([zone_speed, slab_speed]))
```

```python
import math

import jax
import jax.numpy as jnp
import numpy as np
from jax import lax
from jax.experimental import pallas as pl
from jax.experimental.pallas import tpu as pltpu
from jax.sharding import PartitionSpec as P

time_step = 0.1
bond_scale = 1.0


def with_halo(block, sides, width):
    for axis, dim in sides:
        count = lax.axis_size(axis)
        forward = [(i, i + 1) for i in range(count - 1)]
        backward = [(target, source) for source, target in forward]
        low = lax.ppermute(
            lax.slice_in_dim(block, block.shape[dim] - width, None, axis=dim), axis, forward
        )
        high = lax.ppermute(lax.slice_in_dim(block, 0, width, axis=dim), axis, backward)
        block = jnp.concatenate([low, block, high], axis=dim)
    return block


def passed_along(block, axis, distance):
    devices = range(lax.axis_size(axis))
    route = [(i - distance, i) for i in devices if i - distance in devices]
    return lax.ppermute(block, axis, route)


def half_offsets():
    table = []
    for delta_x in range(-3, 4):
        for delta_y in range(-3, 4):
            for delta_z in range(-3, 4):
                radius = delta_x * delta_x + delta_y * delta_y + delta_z * delta_z
                if 0 < radius <= 9 and (delta_x, delta_y, delta_z) > (0, 0, 0):
                    table.append((delta_x, delta_y, delta_z))
    return table


def hex_stiffness():
    poisson = 0.3
    lame_first = poisson / ((1.0 + poisson) * (1.0 - 2.0 * poisson))
    shear_modulus = 0.5 / (1.0 + poisson)
    elastic = np.zeros((6, 6))
    elastic[:3, :3] = lame_first
    for axis_id in range(3):
        elastic[axis_id, axis_id] += 2.0 * shear_modulus
        elastic[3 + axis_id, 3 + axis_id] = shear_modulus
    points = [0.5 - 0.5 / math.sqrt(3.0), 0.5 + 0.5 / math.sqrt(3.0)]
    result = np.zeros((24, 24))
    shear_pairs = ((0, 1), (1, 2), (0, 2))
    for along_x in points:
        for along_y in points:
            for along_z in points:
                coords = (along_x, along_y, along_z)
                gradients = np.zeros((3, 8))
                for corner in range(8):
                    corner_bits = (corner >> 2 & 1, corner >> 1 & 1, corner & 1)
                    factors = [
                        coords[axis_id] if corner_bits[axis_id] else 1.0 - coords[axis_id]
                        for axis_id in range(3)
                    ]
                    slopes = [1.0 if corner_bits[axis_id] else -1.0 for axis_id in range(3)]
                    gradients[0, corner] = slopes[0] * factors[1] * factors[2]
                    gradients[1, corner] = factors[0] * slopes[1] * factors[2]
                    gradients[2, corner] = factors[0] * factors[1] * slopes[2]
                strain = np.zeros((6, 24))
                for axis_id in range(3):
                    strain[axis_id, axis_id * 8 : axis_id * 8 + 8] = gradients[axis_id]
                for shear_row, pair in enumerate(shear_pairs):
                    left_axis, right_axis = pair
                    strain[3 + shear_row, left_axis * 8 : left_axis * 8 + 8] = gradients[right_axis]
                    strain[3 + shear_row, right_axis * 8 : right_axis * 8 + 8] = gradients[
                        left_axis
                    ]
                result += strain.T @ elastic @ strain / 8.0
    return result


def bond_kernel(values_ref, words_ref, out_ref, values_roll, words_roll):
    size_x, size_y, depth = out_ref.shape[1:]

    def roll_row(row, carry):
        for slot in range(7):
            shift = (3 - slot) % depth
            for item in range(4):
                values = values_ref[item, row]
                values_roll[slot, item, row] = (
                    pltpu.roll(values, shift, 1) if shift else values
                )
            for item in range(2):
                words = words_ref[item, row]
                words_roll[slot, item, row] = pltpu.roll(words, shift, 1) if shift else words
        return carry

    lax.fori_loop(0, values_ref.shape[1], roll_row, 0)

    def one_row(row, carry):
        rows_y = pl.ds(3, size_y)
        centre = [values_ref[item, row + 3, rows_y, :] for item in range(4)]
        centre_words = [words_ref[item, row + 3, rows_y, :] for item in range(2)]
        sums = [jnp.zeros_like(centre[0]) for _ in range(3)]
        for number, offset in enumerate(half_offsets()):
            word_id, bit = number // 31, 1 << (number % 31)
            factor = 0.5 * bond_scale / float(sum(d * d for d in offset)) ** 1.5
            for sign in (1, -1):
                delta = [sign * d for d in offset]
                slot, place = delta[2] + 3, (row + 3 + delta[0], pl.ds(3 + delta[1], size_y))
                far = {
                    item: values_roll[(slot, item) + place]
                    for item in range(4)
                    if item == 3 or delta[item]
                }
                if sign > 0:
                    words = centre_words[word_id]
                else:
                    words = words_roll[(slot, word_id) + place]
                projection = None
                for item in range(3):
                    if delta[item]:
                        term = (far[item] - centre[item]) * (factor * delta[item])
                        projection = term if projection is None else projection + term
                strength = jnp.where(
                    (words & bit) != 0, (centre[3] + far[3]) * projection, 0.0
                )
                for item in range(3):
                    if delta[item]:
                        sums[item] = sums[item] + strength * float(delta[item])
        for item in range(3):
            out_ref[item, row] = sums[item]
        return carry

    lax.fori_loop(0, size_x, one_row, 0)


def bond_sum(extended, words_rim, modulus_rim, size_x, size_y, size_z):
    tail = -extended.shape[2] % 8
    room = ((0, 0), (0, 0), (0, tail), (0, 0))
    values = jnp.pad(jnp.concatenate([extended, modulus_rim[None]]), room)
    words = jnp.pad(words_rim, room)
    return pl.pallas_call(
        bond_kernel,
        out_shape=jax.ShapeDtypeStruct((3, size_x, size_y, size_z), jnp.float32),
        scratch_shapes=[
            pltpu.VMEM((7,) + values.shape, jnp.float32),
            pltpu.VMEM((7,) + words.shape, jnp.int32),
        ],
        compiler_params=pltpu.CompilerParams(vmem_limit_bytes=32 * 1024 * 1024),
    )(values, words)


def couple(below_top, map_layers):
    coupled = jnp.zeros_like(below_top)
    for layer_id in range(below_top.shape[3]):
        coupled = coupled + jnp.where(
            map_layers[None] == layer_id, below_top[..., layer_id : layer_id + 1], 0.0
        )
    return coupled


def spread(reaction, map_layers):
    columns = []
    for layer_id in range(reaction.shape[3]):
        columns.append(jnp.sum(jnp.where(map_layers[None] == layer_id, reaction, 0.0), axis=3))
    return jnp.stack(columns, axis=3)


def slab_forces(extended, modulus_rim, start_x, start_y, full_x, full_y, rows_x, rows_y, depth_z):
    stiffness = jnp.asarray(hex_stiffness(), dtype=jnp.float32)
    field_pad = jnp.pad(extended, ((0, 0), (0, 0), (0, 0), (0, 1)))
    pieces = []
    for component in range(3):
        for corner in range(8):
            corner_x, corner_y, corner_z = (corner >> 2 & 1, corner >> 1 & 1, corner & 1)
            pieces.append(
                field_pad[
                    component,
                    2 + corner_x : 3 + corner_x + rows_x,
                    2 + corner_y : 3 + corner_y + rows_y,
                    corner_z : corner_z + depth_z,
                ]
            )
    gathered = jnp.stack(pieces).reshape(24, -1)
    global_x = start_x - 1 + jnp.arange(rows_x + 1)
    global_y = start_y - 1 + jnp.arange(rows_y + 1)
    inside = (
        ((global_x >= 0) & (global_x < full_x - 1))[:, None, None]
        & ((global_y >= 0) & (global_y < full_y - 1))[None, :, None]
        & (jnp.arange(depth_z) < depth_z - 1)[None, None, :]
    ).astype(jnp.float32)
    element_modulus = modulus_rim[2 : 3 + rows_x, 2 : 3 + rows_y, :] * inside
    result = jnp.dot(
        stiffness, gathered, precision=lax.Precision.HIGHEST, preferred_element_type=jnp.float32
    )
    result = result.reshape(24, rows_x + 1, rows_y + 1, depth_z) * element_modulus[None]
    result_pad = jnp.pad(result, ((0, 0), (0, 0), (0, 0), (1, 0)))
    forces = []
    for component in range(3):
        summed = jnp.zeros((rows_x, rows_y, depth_z), jnp.float32)
        for corner in range(8):
            corner_x, corner_y, corner_z = (corner >> 2 & 1, corner >> 1 & 1, corner & 1)
            summed = (
                summed
                - result_pad[
                    component * 8 + corner,
                    1 - corner_x : 1 - corner_x + rows_x,
                    1 - corner_y : 1 - corner_y + rows_y,
                    1 - corner_z : 1 - corner_z + depth_z,
                ]
            )
        forces.append(summed)
    return jnp.stack(forces)


def per_device(displacement, velocity, modulus, bond_words, coupling_map):
    rows_x, rows_y, depth_z = (displacement.shape[2], displacement.shape[3], displacement.shape[4])
    layers = coupling_map.shape[0]
    full_x = rows_x * lax.axis_size("gx")
    full_y = rows_y * lax.axis_size("gy")
    start_x = lax.axis_index("gx") * rows_x
    start_y = lax.axis_index("gy") * rows_y
    is_zone = lax.axis_index("group") == 0
    words_rim = with_halo(bond_words, (("gx", 1), ("gy", 2)), 3)
    modulus_rim = with_halo(modulus[0], (("gx", 0), ("gy", 1)), 3)
    map_layers = jnp.transpose(coupling_map, (1, 2, 0))
    layer_ids = jnp.arange(depth_z)
    moving = (layer_ids >= layers)[None, None, None, :]
    unclamped = (layer_ids > 0)[None, None, None, :]
    position_x = start_x + jnp.arange(rows_x)
    position_y = start_y + jnp.arange(rows_y)
    count_x = (position_x > 0).astype(jnp.float32) + (position_x < full_x - 1).astype(jnp.float32)
    count_y = (position_y > 0).astype(jnp.float32) + (position_y < full_y - 1).astype(jnp.float32)
    count_z = (layer_ids > 0).astype(jnp.float32) + (layer_ids < depth_z - 1).astype(jnp.float32)
    lumped_mass = count_x[:, None, None] * count_y[None, :, None] * count_z[None, None, :] / 8.0
    current = displacement[0]
    velocity_now = velocity[0]
    below_top = passed_along(current[:, :, :, depth_z - layers :], "group", -1)
    coupled = couple(below_top, map_layers)
    current = jnp.where(
        is_zone, jnp.concatenate([coupled, current[:, :, :, layers:]], axis=3), current
    )
    extended = with_halo(current, (("gx", 1), ("gy", 2)), 3)

    def zone_branch():
        return bond_sum(extended, words_rim, modulus_rim, rows_x, rows_y, depth_z)

    def slab_branch():
        return slab_forces(
            extended, modulus_rim, start_x, start_y, full_x, full_y, rows_x, rows_y, depth_z
        )

    forces = lax.cond(is_zone, zone_branch, slab_branch)
    reaction = passed_along(forces[:, :, :, :layers], "group", 1)
    interface = jnp.pad(
        spread(reaction, map_layers), ((0, 0), (0, 0), (0, 0), (depth_z - layers, 0))
    )
    slab_total = forces + interface
    zone_velocity = jnp.where(moving, velocity_now + time_step * forces, velocity_now)
    zone_field = jnp.where(moving, current + time_step * zone_velocity, current)
    slab_velocity = jnp.where(unclamped, velocity_now + time_step * slab_total / lumped_mass, 0.0)
    slab_field = jnp.where(unclamped, current + time_step * slab_velocity, 0.0)
    velocity_now = jnp.where(is_zone, zone_velocity, slab_velocity)
    current = jnp.where(is_zone, zone_field, slab_field)
    return (current[None], velocity_now[None])


def solution(mesh):
    return jax.shard_map(
        per_device,
        mesh=mesh,
        in_specs=(
            P("group", None, "gx", "gy", None),
            P("group", None, "gx", "gy", None),
            P("group", "gx", "gy", None),
            P(None, "gx", "gy", None),
            P(None, "gx", "gy"),
        ),
        out_specs=(P("group", None, "gx", "gy", None), P("group", None, "gx", "gy", None)),
        check_vma=False,
    )
```
